32 devices in a mesh: blk: 16 (over z, y, x), col: 2 (over core).
Axes of the slice: x: 2, y: 2, z: 4, core: 2. Of those that a mesh axis runs over, the one named last changes fastest.
Arguments:
- queries: bfloat16 [128, 16384], P('blk', 'col'), may hold values from -6 to 6
- factor: bfloat16 [16384, 1024], P('col', 'blk'), may hold values from -0.046875 to 0.046875
- eigenvalues: float32 [1024], replicated, may hold values from 0.05 to 20
- damping: float32 [1], replicated, may hold values from 0.5 to 2
- train_rows: bfloat16 [16384, 16384], P('blk', 'col'), may hold values from -0.046875 to 0.046875
Outputs:
- scores: bfloat16 [128, 16384], P('col', 'blk')
The draws below stay inside these ranges and needn't reach their ends.
All inputs are finite; a program needn't handle non-finite values.
Results may differ from the reference program's by a relative error of at most 0.0049.
Values may be sent and summed in bfloat16 or wider, within the bound.
A program may use at most 64 MiB of HBM per device.

```python
import math
import jax
import jax.numpy as jnp
from jax import lax

PROJ = 16384
RANK = 1024
TR_DEV = 1024
QUERIES = 128
TRAIN = 16384
N_BLK = 16


def block_scale(key, dims, shards, smallest, high):
    loudness = 1.0
    for position, shards_of in shards:
        heights = jax.random.uniform(jax.random.fold_in(jax.random.fold_in(key, 6), position), (shards_of,), jnp.float32, smallest / len(shards), high / len(shards))
        loudness = loudness * jnp.repeat(jnp.exp(heights), dims[position] // shards_of).reshape((-1,) + (1,) * (len(dims) - 1 - position))
    return loudness


def centred(rng, dims, deviation, most, shards=(), dtype=jnp.bfloat16):
    level = block_scale(rng, dims, shards, -0.22, 0.18) if shards else 1.0
    array = jax.random.normal(rng, dims, jnp.float32) * deviation * level
    return jnp.minimum(jnp.maximum(array, -most), most).astype(dtype)


def setup_inputs(seed: int = 0) -> dict:
    key_of = jax.random.split(jax.random.key(seed), 6)
    return {
        "queries": centred(key_of[0], (QUERIES, PROJ), 1.0, 6.0, ((0, 16), (1, 2))),
        "factor": centred(key_of[1], (PROJ, RANK), PROJ ** -0.5, 0.046875, ((0, 2), (1, 16))),
        "eigenvalues": jnp.clip(jnp.exp(jax.random.uniform(key_of[2], (RANK,), jnp.float32, math.log(0.05), math.log(20.0))), 0.05, 20.0),
        "damping": jnp.clip(jnp.exp(jax.random.uniform(key_of[3], (1,), jnp.float32, math.log(0.5), math.log(2.0))), 0.5, 2.0),
        "train_rows": centred(key_of[4], (TRAIN, PROJ), PROJ ** -0.5, 0.046875, ((0, 16), (1, 2))),
    }


def reference(queries, factor, eigenvalues, damping, train_rows):
    damp_value = damping[0]
    weights = eigenvalues / (eigenvalues + damp_value)
    coefficient = jnp.dot(queries, factor, preferred_element_type=jnp.float32)
    scaled = coefficient * weights[None, :]
    correction = jnp.dot(scaled, factor.astype(jnp.float32).T, precision=lax.Precision.HIGHEST)
    preconditioned = ((queries.astype(jnp.float32) - correction) / damp_value).astype(jnp.bfloat16)
    blocks = train_rows.reshape(N_BLK, TR_DEV, PROJ)

    def one_block(block_rows):
        return jnp.dot(preconditioned, block_rows.T, preferred_element_type=jnp.float32).astype(jnp.bfloat16)

    result = lax.map(one_block, blocks)
    return jnp.transpose(result, (1, 0, 2)).reshape(QUERIES, TRAIN)
```

```python
import jax
import jax.numpy as jnp
from jax import lax
from jax.sharding import PartitionSpec as P


def per_device(queries, factor, eigenvalues, damping, train_rows):
    damp_value = damping[0]
    weights = eigenvalues / (eigenvalues + damp_value)
    query_part = lax.all_to_all(queries, "blk", split_axis=1, concat_axis=0, tiled=True)
    factor_part = lax.all_to_all(factor, "blk", split_axis=0, concat_axis=1, tiled=True)
    partial_value = jnp.dot(query_part, factor_part, preferred_element_type=jnp.float32)
    coefficient = lax.psum(partial_value, ("blk", "col"))
    scaled = coefficient * weights[None, :]
    correction = jnp.dot(scaled, factor_part.astype(jnp.float32).T, precision=lax.Precision.HIGHEST)
    pre_part = ((query_part.astype(jnp.float32) - correction) / damp_value).astype(jnp.bfloat16)
    pre_all = lax.all_gather(pre_part, "blk", axis=1, tiled=True)
    partial_scores = jnp.einsum("qk,nk->qn", pre_all, train_rows, preferred_element_type=jnp.float32)
    scores = lax.psum_scatter(partial_scores, "col", scatter_dimension=0, tiled=True)
    return scores.astype(jnp.bfloat16)


def solution(mesh):
    in_specs = (P("blk", "col"), P("col", "blk"), P(), P(), P("blk", "col"))
    out_specs = P("col", "blk")
    return jax.shard_map(
        per_device, mesh=mesh, in_specs=in_specs, out_specs=out_specs, check_vma=False
    )
```

```python
import functools

import jax
import jax.numpy as jnp
from jax import lax
from jax.experimental import pallas as pl
from jax.experimental.pallas import tpu as pltpu
from jax.sharding import PartitionSpec as P

MESH = pl.DeviceIdType.MESH
CONTRACT_LAST = (((1,), (1,)), ((), ()))


def fused_kernel(
    nb, queries, factor_t, eigenvalues, damping, train_rows, out,
    query_in, factor_in, train_in, part, part_in, half_sum, half_in, scaled_out, scaled_in,
    pre, total, total_in,
    train_sem, own_sem, query_send, query_recv, factor_send, factor_recv,
    part_send, part_recv, scaled_send, scaled_recv, pre_send, pre_recv, pair_send, pair_recv,
):
    me = lax.axis_index("blk")
    side = lax.axis_index("col")
    rows, width = query_in.shape[1], query_in.shape[2]
    rank = eigenvalues.shape[1]
    every = nb * rows
    half = every // 2

    def span(index):
        return pl.ds(pl.multiple_of(index * width, width), width)

    def to_peer(source, target, send_sem, recv_sem, peer):
        return pltpu.make_async_remote_copy(
            src_ref=source, dst_ref=target, send_sem=send_sem, recv_sem=recv_sem,
            device_id={"blk": peer}, device_id_type=MESH,
        )

    def to_pair(source, target, index):
        return pltpu.make_async_remote_copy(
            src_ref=source, dst_ref=target,
            send_sem=pair_send.at[index], recv_sem=pair_recv.at[index],
            device_id={"col": 1 - side}, device_id_type=MESH,
        )

    def each_peer(body):
        def step(k, carry):
            body(lax.rem(me + k, nb))
            return carry
        lax.fori_loop(1, nb, step, 0)

    def query_copy(source, peer):
        return to_peer(queries.at[:, span(peer)], query_in.at[source],
                       query_send.at[peer], query_recv.at[source], peer)

    def factor_copy(source, peer):
        return to_peer(factor_t.at[:, span(peer)], factor_in.at[source],
                       factor_send.at[peer], factor_recv.at[source], peer)

    def part_copy(source, peer):
        return to_peer(part.at[peer], part_in.at[source],
                       part_send.at[peer], part_recv.at[source], peer)

    def scaled_copy(source, peer):
        return to_peer(scaled_out, scaled_in.at[source],
                       scaled_send.at[peer], scaled_recv.at[source], peer)

    def pre_copy(source, peer):
        return to_peer(pre.at[source], pre.at[source],
                       pre_send.at[peer], pre_recv.at[source], peer)

    def train_copy(index):
        return pltpu.make_async_copy(
            train_rows.at[:, span(index)], train_in.at[index], train_sem.at[index])

    own_query = pltpu.make_async_copy(queries.at[:, span(me)], query_in.at[me], own_sem.at[0])
    own_factor = pltpu.make_async_copy(factor_t.at[:, span(me)], factor_in.at[me], own_sem.at[1])

    barrier = pltpu.get_barrier_semaphore()
    each_peer(lambda peer: pl.semaphore_signal(
        barrier, inc=1, device_id={"blk": peer}, device_id_type=MESH))
    pl.semaphore_signal(barrier, inc=1, device_id={"col": 1 - side}, device_id_type=MESH)
    pl.semaphore_wait(barrier, nb)

    own_query.start()
    own_factor.start()
    each_peer(lambda peer: query_copy(me, peer).start())
    each_peer(lambda peer: factor_copy(me, peer).start())

    def start_train(k, carry):
        train_copy(lax.rem(me + nb - k, nb)).start()
        return carry
    lax.fori_loop(0, nb, start_train, 0)

    own_query.wait()
    own_factor.wait()
    each_peer(lambda peer: query_copy(peer, peer).wait_recv())
    each_peer(lambda peer: factor_copy(peer, peer).wait_recv())

    query_wide = query_in[...].astype(jnp.float32).reshape(every, width)
    factor_slice = factor_in[...].reshape(rank, width)
    partial_value = lax.dot_general(
        query_wide.astype(jnp.bfloat16), factor_slice, CONTRACT_LAST,
        preferred_element_type=jnp.float32)
    part[...] = partial_value.reshape(nb, rows, rank)

    each_peer(lambda peer: part_copy(me, peer).start())
    part_in[me] = part[me]
    each_peer(lambda peer: part_copy(peer, peer).wait_recv())
    half_sum[...] = jnp.sum(part_in[...], axis=0)
    exchange = to_pair(half_sum, half_in, 0)
    exchange.start()
    weights = eigenvalues[...] / (eigenvalues[...] + damping[0])
    exchange.wait()
    scaled_out[...] = (half_sum[...] + half_in[...]) * weights
    each_peer(lambda peer: scaled_copy(me, peer).start())
    scaled_in[me] = scaled_out[...]
    each_peer(lambda peer: scaled_copy(peer, peer).wait_recv())

    scaled = scaled_in[...].reshape(every, rank)
    first = scaled.astype(jnp.bfloat16)
    rest = scaled - first.astype(jnp.float32)
    second = rest.astype(jnp.bfloat16)
    third = (rest - second.astype(jnp.float32)).astype(jnp.bfloat16)
    factor_slice = factor_in[...].reshape(rank, width)
    correction = (
        jnp.dot(third, factor_slice, preferred_element_type=jnp.float32)
        + jnp.dot(second, factor_slice, preferred_element_type=jnp.float32)
    ) + jnp.dot(first, factor_slice, preferred_element_type=jnp.float32)
    query_wide = query_in[...].astype(jnp.float32).reshape(every, width)
    pre[me] = ((query_wide - correction) / damping[0]).astype(jnp.bfloat16)

    each_peer(lambda peer: pre_copy(me, peer).start())

    def scores_of(index):
        train_copy(index).wait()
        return lax.dot_general(
            pre[index], train_in[index], CONTRACT_LAST, preferred_element_type=jnp.float32)

    total[...] = scores_of(me)

    def score_step(k, carry):
        source = lax.rem(me + nb - k, nb)
        pre_copy(source, source).wait_recv()
        total[...] += scores_of(source)
        return carry
    lax.fori_loop(1, nb, score_step, 0)

    other_rows = pl.ds(pl.multiple_of((1 - side) * half, half), half)
    own_rows = pl.ds(pl.multiple_of(side * half, half), half)
    last = to_pair(total.at[other_rows], total_in, 1)
    last.start()

    def finish(peer):
        query_copy(me, peer).wait_send()
        factor_copy(me, peer).wait_send()
        part_copy(me, peer).wait_send()
        scaled_copy(me, peer).wait_send()
        pre_copy(me, peer).wait_send()
    each_peer(finish)
    last.wait()
    out[...] = (total[own_rows, :] + total_in[...]).astype(out.dtype)


def fused(nb, queries, factor, eigenvalues, damping, train_rows):
    rows, depth = queries.shape
    rank_slice = factor.shape[1]
    width = depth // nb
    rank = eigenvalues.shape[0]
    every = nb * rows
    train = train_rows.shape[0]
    anywhere = pl.BlockSpec(memory_space=pl.ANY)
    vmem = pl.BlockSpec(memory_space=pltpu.VMEM)
    dma = pltpu.SemaphoreType.DMA
    f32, bf16 = jnp.float32, jnp.bfloat16
    return pl.pallas_call(
        functools.partial(fused_kernel, nb),
        out_shape=jax.ShapeDtypeStruct((every // 2, train), bf16),
        in_specs=[anywhere, anywhere, vmem, pl.BlockSpec(memory_space=pltpu.SMEM), anywhere],
        out_specs=vmem,
        scratch_shapes=[
            pltpu.VMEM((nb, rows, width), bf16),
            pltpu.VMEM((nb, rank_slice, width), bf16),
            pltpu.VMEM((nb, train, width), bf16),
            pltpu.VMEM((nb, rows, rank), f32),
            pltpu.VMEM((nb, rows, rank), f32),
            pltpu.VMEM((rows, rank), f32),
            pltpu.VMEM((rows, rank), f32),
            pltpu.VMEM((rows, rank), f32),
            pltpu.VMEM((nb, rows, rank), f32),
            pltpu.VMEM((nb, every, width), bf16),
            pltpu.VMEM((every, train), f32),
            pltpu.VMEM((every // 2, train), f32),
            dma((nb,)), dma((2,)),
            dma((nb,)), dma((nb,)), dma((nb,)), dma((nb,)),
            dma((nb,)), dma((nb,)), dma((nb,)), dma((nb,)),
            dma((nb,)), dma((nb,)), dma((2,)), dma((2,)),
        ],
        compiler_params=pltpu.CompilerParams(
            collective_id=0, has_side_effects=True, vmem_limit_bytes=56 * 1024 * 1024),
    )(queries, factor.T, eigenvalues[None, :], damping, train_rows)


def plain(queries, factor, eigenvalues, damping, train_rows):
    damp_value = damping[0]
    weights = eigenvalues / (eigenvalues + damp_value)
    query_part = lax.all_to_all(queries, "blk", split_axis=1, concat_axis=0, tiled=True)
    factor_part = lax.all_to_all(factor, "blk", split_axis=0, concat_axis=1, tiled=True)
    partial_value = jnp.dot(query_part, factor_part, preferred_element_type=jnp.float32)
    coefficient = lax.psum(partial_value, ("blk", "col"))
    scaled = coefficient * weights[None, :]
    correction = jnp.dot(scaled, factor_part.astype(jnp.float32).T, precision=lax.Precision.HIGHEST)
    pre_part = ((query_part.astype(jnp.float32) - correction) / damp_value).astype(jnp.bfloat16)
    pre_all = lax.all_gather(pre_part, "blk", axis=1, tiled=True)
    partial_scores = jnp.einsum("qk,nk->qn", pre_all, train_rows, preferred_element_type=jnp.float32)
    scores = lax.psum_scatter(partial_scores, "col", scatter_dimension=0, tiled=True)
    return scores.astype(jnp.bfloat16)


def per_device(nb, pair, queries, factor, eigenvalues, damping, train_rows):
    rows, depth = queries.shape
    width = depth // nb
    fits = pair == 2 and width % 128 == 0 and rows % 8 == 0 and factor.shape[1] % 16 == 0
    if fits:
        return fused(nb, queries, factor, eigenvalues, damping, train_rows)
    return plain(queries, factor, eigenvalues, damping, train_rows)


def solution(mesh):
    in_specs = (P("blk", "col"), P("col", "blk"), P(), P(), P("blk", "col"))
    out_specs = P("col", "blk")
    body = functools.partial(per_device, mesh.shape["blk"], mesh.shape["col"])
    return jax.shard_map(
        body, mesh=mesh, in_specs=in_specs, out_specs=out_specs, check_vma=False
    )
```

```python
import functools

import jax
import jax.numpy as jnp
from jax import lax
from jax.experimental import pallas as pl
from jax.experimental.pallas import tpu as pltpu
from jax.sharding import PartitionSpec as P

MESH = pl.DeviceIdType.MESH
CONTRACT_LAST = (((1,), (1,)), ((), ()))


def fused_kernel(
    nb, queries, factor_t, eigenvalues, damping, train_rows, out,
    query_in, factor_in, train_in, part, pair_in, part_sum, part_in, scaled_out, scaled_in,
    pre, total, total_in,
    train_sem, own_sem, query_send, query_recv, factor_send, factor_recv,
    part_send, part_recv, scaled_send, scaled_recv, line_send, line_recv,
    side_send, side_recv, corner_send, corner_recv, pair_send, pair_recv,
):
    me = lax.axis_index("blk")
    side = lax.axis_index("col")
    rows, width = query_in.shape[1], query_in.shape[2]
    rank = eigenvalues.shape[1]
    every = nb * rows
    half = every // 2
    half_rank = rank // 2
    line = nb // 4
    px, py, pz = lax.rem(me, 2), lax.rem(lax.div(me, 2), 2), lax.div(me, 4)
    next_x = me + 1 - 2 * px
    next_y = me + 2 - 4 * py

    def span(index):
        return pl.ds(pl.multiple_of(index * width, width), width)

    def to_peer(source, target, send_sem, recv_sem, peer):
        return pltpu.make_async_remote_copy(
            src_ref=source, dst_ref=target, send_sem=send_sem, recv_sem=recv_sem,
            device_id={"blk": peer}, device_id_type=MESH,
        )

    def to_pair(source, target, index):
        return pltpu.make_async_remote_copy(
            src_ref=source, dst_ref=target,
            send_sem=pair_send.at[index], recv_sem=pair_recv.at[index],
            device_id={"col": 1 - side}, device_id_type=MESH,
        )

    def each_peer(body):
        def step(k, carry):
            body(lax.rem(me + k, nb))
            return carry
        lax.fori_loop(1, nb, step, 0)

    def query_copy(source, peer):
        return to_peer(queries.at[:, span(peer)], query_in.at[source],
                       query_send.at[peer], query_recv.at[source], peer)

    def factor_copy(source, peer):
        return to_peer(factor_t.at[:, span(peer)], factor_in.at[source],
                       factor_send.at[peer], factor_recv.at[source], peer)

    def part_copy(source, peer):
        return to_peer(part_sum.at[peer], part_in.at[source],
                       part_send.at[peer], part_recv.at[source], peer)

    def scaled_copy(source, peer):
        return to_peer(scaled_out, scaled_in.at[side, source],
                       scaled_send.at[peer], scaled_recv.at[source], peer)

    def block(z, flip_x, flip_y):
        x = 1 - px if flip_x else px
        y = 1 - py if flip_y else py
        return z * 4 + y * 2 + x

    def line_copy(z, up):
        index = block(z, False, False)
        return to_peer(pre.at[index], pre.at[index], line_send.at[up, z], line_recv.at[z],
                       me + (4 if up else -4))

    def side_copy(z, along, incoming=False):
        index = block(z, incoming and along == 0, incoming and along == 1)
        return to_peer(pre.at[index], pre.at[index], side_send.at[along, z],
                       side_recv.at[along, z], next_y if along else next_x)

    def corner_copy(z, along, incoming=False):
        index = block(z, incoming or along == 1, incoming or along == 0)
        rows_of = pl.ds((1 - along) * half, half)
        return to_peer(pre.at[index, rows_of], pre.at[index, rows_of], corner_send.at[along, z],
                       corner_recv.at[along, z], next_y if along else next_x)

    def train_copy(index):
        return pltpu.make_async_copy(
            train_rows.at[:, span(index)], train_in.at[index], train_sem.at[index])

    own_query = pltpu.make_async_copy(queries.at[:, span(me)], query_in.at[me], own_sem.at[0])
    own_factor = pltpu.make_async_copy(factor_t.at[:, span(me)], factor_in.at[me], own_sem.at[1])

    barrier = pltpu.get_barrier_semaphore()
    each_peer(lambda peer: pl.semaphore_signal(
        barrier, inc=1, device_id={"blk": peer}, device_id_type=MESH))
    pl.semaphore_signal(barrier, inc=1, device_id={"col": 1 - side}, device_id_type=MESH)
    pl.semaphore_wait(barrier, nb)

    own_query.start()
    own_factor.start()
    each_peer(lambda peer: query_copy(me, peer).start())
    each_peer(lambda peer: factor_copy(me, peer).start())

    def start_train(k, carry):
        train_copy(lax.rem(me + nb - k, nb)).start()
        return carry
    lax.fori_loop(0, nb, start_train, 0)

    own_query.wait()
    own_factor.wait()
    each_peer(lambda peer: query_copy(peer, peer).wait_recv())
    each_peer(lambda peer: factor_copy(peer, peer).wait_recv())

    query_wide = query_in[...].astype(jnp.float32).reshape(every, width)
    factor_slice = factor_in[...].reshape(rank, width)
    partial_value = lax.dot_general(
        query_wide.astype(jnp.bfloat16), factor_slice, CONTRACT_LAST,
        preferred_element_type=jnp.float32)
    for k in range(2):
        part[k] = partial_value[:, k * half_rank:(k + 1) * half_rank].reshape(nb, rows, half_rank)

    exchange = to_pair(part.at[1 - side], pair_in, 0)
    exchange.start()
    own_rank = pl.ds(pl.multiple_of(side * half_rank, half_rank), half_rank)
    own_values = eigenvalues[:, own_rank]
    weights = own_values / (own_values + damping[0])
    exchange.wait()
    part_sum[...] = part[side] + pair_in[...]
    each_peer(lambda peer: part_copy(me, peer).start())
    part_in[me] = part_sum[me]
    each_peer(lambda peer: part_copy(peer, peer).wait_recv())
    scaled_out[...] = jnp.sum(part_in[...], axis=0) * weights
    each_peer(lambda peer: scaled_copy(me, peer).start())
    scaled_in[side, me] = scaled_out[...]
    each_peer(lambda peer: scaled_copy(peer, peer).wait_recv())
    swap = to_pair(scaled_in.at[side], scaled_in.at[side], 2)
    swap.start()

    def correction_of(which):
        scaled = scaled_in[which].reshape(every, half_rank)
        first = scaled.astype(jnp.bfloat16)
        rest = scaled - first.astype(jnp.float32)
        second = rest.astype(jnp.bfloat16)
        third = (rest - second.astype(jnp.float32)).astype(jnp.bfloat16)
        slots = nb // 2
        factor_half = factor_in[pl.ds(which * slots, slots)].reshape(half_rank, width)
        return (
            jnp.dot(third, factor_half, preferred_element_type=jnp.float32)
            + jnp.dot(second, factor_half, preferred_element_type=jnp.float32)
        ) + jnp.dot(first, factor_half, preferred_element_type=jnp.float32)

    correction = correction_of(side)
    swap.wait()
    correction = correction + correction_of(1 - side)
    query_wide = query_in[...].astype(jnp.float32).reshape(every, width)
    pre[me] = ((query_wide - correction) / damping[0]).astype(jnp.bfloat16)

    def scores_of(index):
        train_copy(index).wait()
        return lax.dot_general(
            pre[index], train_in[index], CONTRACT_LAST, preferred_element_type=jnp.float32)

    def height(i):
        mirror = lax.div(pz, line // 2)
        near = pz + mirror * (line - 1 - 2 * pz)
        v = near + i * (1 - 2 * near) if i < 2 else i
        return v + mirror * (line - 1 - 2 * v)

    def pass_on(z):
        @pl.when((z <= pz) & (pz < line - 1))
        def _():
            line_copy(z, 1).start()

        @pl.when((z >= pz) & (pz > 0))
        def _():
            line_copy(z, 0).start()

    total[...] = jnp.zeros_like(total)
    for i in range(line + 2):
        if i < line:
            z = height(i)
            if i > 0:
                line_copy(z, 1).wait_recv()
            pass_on(z)
            side_copy(z, 0).start()
            side_copy(z, 1).start()
        if 1 <= i <= line:
            z = height(i - 1)
            side_copy(z, 0, True).wait_recv()
            corner_copy(z, 1).start()
            side_copy(z, 1, True).wait_recv()
            corner_copy(z, 0).start()
        if i >= 2:
            z = height(i - 2)
            corner_copy(z, 0, True).wait_recv()
            corner_copy(z, 1, True).wait_recv()
            for flip_x in (False, True):
                for flip_y in (False, True):
                    total[...] += scores_of(block(z, flip_x, flip_y))

    other_rows = pl.ds(pl.multiple_of((1 - side) * half, half), half)
    own_rows = pl.ds(pl.multiple_of(side * half, half), half)
    last = to_pair(total.at[other_rows], total_in, 1)
    last.start()

    def finish(peer):
        query_copy(me, peer).wait_send()
        factor_copy(me, peer).wait_send()
        part_copy(me, peer).wait_send()
        scaled_copy(me, peer).wait_send()
    each_peer(finish)
    for i in range(line):
        z = height(i)

        @pl.when((z <= pz) & (pz < line - 1))
        def _():
            line_copy(z, 1).wait_send()

        @pl.when((z >= pz) & (pz > 0))
        def _():
            line_copy(z, 0).wait_send()

        for along in range(2):
            side_copy(z, along).wait_send()
            corner_copy(z, along).wait_send()
    last.wait()
    out[...] = (total[own_rows, :] + total_in[...]).astype(out.dtype)


def fused(nb, queries, factor, eigenvalues, damping, train_rows):
    rows, depth = queries.shape
    rank_slice = factor.shape[1]
    width = depth // nb
    rank = eigenvalues.shape[0]
    every = nb * rows
    train = train_rows.shape[0]
    line = nb // 4
    anywhere = pl.BlockSpec(memory_space=pl.ANY)
    vmem = pl.BlockSpec(memory_space=pltpu.VMEM)
    dma = pltpu.SemaphoreType.DMA
    f32, bf16 = jnp.float32, jnp.bfloat16
    return pl.pallas_call(
        functools.partial(fused_kernel, nb),
        out_shape=jax.ShapeDtypeStruct((every // 2, train), bf16),
        in_specs=[anywhere, anywhere, vmem, pl.BlockSpec(memory_space=pltpu.SMEM), anywhere],
        out_specs=vmem,
        scratch_shapes=[
            pltpu.VMEM((nb, rows, width), bf16),
            pltpu.VMEM((nb, rank_slice, width), bf16),
            pltpu.VMEM((nb, train, width), bf16),
            pltpu.VMEM((2, nb, rows, rank // 2), f32),
            pltpu.VMEM((nb, rows, rank // 2), f32),
            pltpu.VMEM((nb, rows, rank // 2), f32),
            pltpu.VMEM((nb, rows, rank // 2), f32),
            pltpu.VMEM((rows, rank // 2), f32),
            pltpu.VMEM((2, nb, rows, rank // 2), f32),
            pltpu.VMEM((nb, every, width), bf16),
            pltpu.VMEM((every, train), f32),
            pltpu.VMEM((every // 2, train), f32),
            dma((nb,)), dma((2,)),
            dma((nb,)), dma((nb,)), dma((nb,)), dma((nb,)),
            dma((nb,)), dma((nb,)), dma((nb,)), dma((nb,)),
            dma((2, line)), dma((line,)), dma((2, line)), dma((2, line)),
            dma((2, line)), dma((2, line)), dma((3,)), dma((3,)),
        ],
        compiler_params=pltpu.CompilerParams(
            collective_id=0, has_side_effects=True, vmem_limit_bytes=56 * 1024 * 1024),
    )(queries, factor.T, eigenvalues[None, :], damping, train_rows)


def plain(queries, factor, eigenvalues, damping, train_rows):
    damp_value = damping[0]
    weights = eigenvalues / (eigenvalues + damp_value)
    query_part = lax.all_to_all(queries, "blk", split_axis=1, concat_axis=0, tiled=True)
    factor_part = lax.all_to_all(factor, "blk", split_axis=0, concat_axis=1, tiled=True)
    partial_value = jnp.dot(query_part, factor_part, preferred_element_type=jnp.float32)
    coefficient = lax.psum(partial_value, ("blk", "col"))
    scaled = coefficient * weights[None, :]
    correction = jnp.dot(scaled, factor_part.astype(jnp.float32).T, precision=lax.Precision.HIGHEST)
    pre_part = ((query_part.astype(jnp.float32) - correction) / damp_value).astype(jnp.bfloat16)
    pre_all = lax.all_gather(pre_part, "blk", axis=1, tiled=True)
    partial_scores = jnp.einsum("qk,nk->qn", pre_all, train_rows, preferred_element_type=jnp.float32)
    scores = lax.psum_scatter(partial_scores, "col", scatter_dimension=0, tiled=True)
    return scores.astype(jnp.bfloat16)


def per_device(nb, pair, queries, factor, eigenvalues, damping, train_rows):
    rows, depth = queries.shape
    width = depth // nb
    fits = pair == 2 and width % 128 == 0 and rows % 8 == 0 and factor.shape[1] % 16 == 0
    fits = fits and nb == 16
    if fits:
        return fused(nb, queries, factor, eigenvalues, damping, train_rows)
    return plain(queries, factor, eigenvalues, damping, train_rows)


def solution(mesh):
    in_specs = (P("blk", "col"), P("col", "blk"), P(), P(), P("blk", "col"))
    out_specs = P("col", "blk")
    body = functools.partial(per_device, mesh.shape["blk"], mesh.shape["col"])
    return jax.shard_map(
        body, mesh=mesh, in_specs=in_specs, out_specs=out_specs, check_vma=False
    )
```

```python
import functools

import jax
import jax.numpy as jnp
from jax import lax
from jax.experimental import pallas as pl
from jax.experimental.pallas import tpu as pltpu
from jax.sharding import PartitionSpec as P

MESH = pl.DeviceIdType.MESH
CONTRACT_LAST = (((1,), (1,)), ((), ()))


def fused_kernel(
    nb, queries, factor_t, eigenvalues, damping, train_rows, out,
    query_in, factor_in, train_in, part, pair_in, part_sum, part_in, scaled_out, scaled_in,
    cross_out, cross_in, pre, total, total_in,
    train_sem, own_sem, query_send, query_recv, factor_send, factor_recv,
    part_send, part_recv, scaled_send, scaled_recv, line_send, line_recv,
    side_send, side_recv, corner_send, corner_recv, pair_send, pair_recv, cross_send, cross_recv,
):
    me = lax.axis_index("blk")
    side = lax.axis_index("col")
    rows, wide = query_in.shape[1], query_in.shape[2]
    width = wide // 2
    rank = eigenvalues.shape[1]
    every = nb * rows
    half = every // 2
    members = nb // 2
    group, mine = lax.div(me, members), lax.rem(me, members)
    half_rank = rank // 4
    line = nb // 4
    px, py, pz = lax.rem(me, 2), lax.rem(lax.div(me, 2), 2), lax.div(me, 4)
    next_x = me + 1 - 2 * px
    next_y = me + 2 - 4 * py

    def span(index, size):
        return pl.ds(pl.multiple_of(index * size, size), size)

    def to_peer(source, target, send_sem, recv_sem, peer):
        return pltpu.make_async_remote_copy(
            src_ref=source, dst_ref=target, send_sem=send_sem, recv_sem=recv_sem,
            device_id={"blk": peer}, device_id_type=MESH,
        )

    def to_pair(source, target, index):
        return pltpu.make_async_remote_copy(
            src_ref=source, dst_ref=target,
            send_sem=pair_send.at[index], recv_sem=pair_recv.at[index],
            device_id={"col": 1 - side}, device_id_type=MESH,
        )

    def each_peer(body):
        def step(k, carry):
            body(lax.rem(me + k, nb))
            return carry
        lax.fori_loop(1, nb, step, 0)

    def each_member(body):
        def step(k, carry):
            body(lax.rem(mine + k, members))
            return carry
        lax.fori_loop(1, members, step, 0)

    def query_copy(source, peer):
        return to_peer(queries.at[:, span(lax.rem(peer, members), wide)], query_in.at[source],
                       query_send.at[peer], query_recv.at[source], peer)

    def factor_copy(source, member):
        return to_peer(factor_t.at[:, span(member, wide)], factor_in.at[source],
                       factor_send.at[member], factor_recv.at[source], group * members + member)

    def part_copy(source, member):
        return to_peer(part_sum.at[member], part_in.at[source],
                       part_send.at[member], part_recv.at[source], group * members + member)

    def scaled_copy(source, member):
        return to_peer(scaled_out, scaled_in.at[side, source],
                       scaled_send.at[member], scaled_recv.at[source], group * members + member)

    def cross_copy(k):
        return to_peer(cross_out.at[k], cross_in.at[k], cross_send.at[k], cross_recv.at[k],
                       (1 - group) * members + mine)

    def block(z, flip_x, flip_y):
        x = 1 - px if flip_x else px
        y = 1 - py if flip_y else py
        return z * 4 + y * 2 + x

    def line_copy(z, k, up):
        half_block = pre.at[block(z, False, False), pl.ds(k * half, half)]
        return to_peer(half_block, half_block, line_send.at[up, 2 * z + k],
                       line_recv.at[2 * z + k], me + (4 if up else -4))

    def side_copy(z, k, along, incoming=False):
        index = block(z, incoming and along == 0, incoming and along == 1)
        half_block = pre.at[index, pl.ds(k * half, half)]
        return to_peer(half_block, half_block, side_send.at[along, 2 * z + k],
                       side_recv.at[along, 2 * z + k], next_y if along else next_x)

    def corner_copy(z, along, incoming=False):
        index = block(z, incoming or along == 1, incoming or along == 0)
        half_block = pre.at[index, pl.ds((1 - along) * half, half)]
        return to_peer(half_block, half_block, corner_send.at[along, z],
                       corner_recv.at[along, z], next_y if along else next_x)

    def train_copy(index):
        chunk = lax.rem(index, members) * 2 + lax.div(index, members)
        return pltpu.make_async_copy(
            train_rows.at[:, span(chunk, width)], train_in.at[index], train_sem.at[index])

    own_query = pltpu.make_async_copy(
        queries.at[:, span(mine, wide)], query_in.at[me], own_sem.at[0])
    own_factor = pltpu.make_async_copy(
        factor_t.at[:, span(mine, wide)], factor_in.at[mine], own_sem.at[1])

    barrier = pltpu.get_barrier_semaphore()
    each_peer(lambda peer: pl.semaphore_signal(
        barrier, inc=1, device_id={"blk": peer}, device_id_type=MESH))
    pl.semaphore_signal(barrier, inc=1, device_id={"col": 1 - side}, device_id_type=MESH)
    pl.semaphore_wait(barrier, nb)

    own_query.start()
    own_factor.start()
    each_peer(lambda peer: query_copy(me, peer).start())
    each_member(lambda peer: factor_copy(mine, peer).start())

    def start_train(k, carry):
        train_copy(lax.rem(me + nb - k, nb)).start()
        return carry
    lax.fori_loop(0, nb, start_train, 0)

    own_query.wait()
    own_factor.wait()
    each_peer(lambda peer: query_copy(peer, peer).wait_recv())
    each_member(lambda peer: factor_copy(peer, peer).wait_recv())

    query_wide = query_in[...].astype(jnp.float32).reshape(every, wide)
    partial_value = lax.dot_general(
        query_wide.astype(jnp.bfloat16), factor_in[...].reshape(2 * half_rank, wide),
        CONTRACT_LAST, preferred_element_type=jnp.float32)
    for k in range(2):
        part[k] = partial_value[:, k * half_rank:(k + 1) * half_rank].reshape(
            members, 2 * rows, half_rank)

    exchange = to_pair(part.at[1 - side], pair_in, 0)
    exchange.start()
    own_rank = span(2 * group + side, half_rank)
    own_values = eigenvalues[:, own_rank]
    weights = own_values / (own_values + damping[0])
    exchange.wait()
    part_sum[...] = part[side] + pair_in[...]
    each_member(lambda peer: part_copy(mine, peer).start())
    part_in[mine] = part_sum[mine]
    each_member(lambda peer: part_copy(peer, peer).wait_recv())
    scaled_out[...] = jnp.sum(part_in[...], axis=0) * weights
    each_member(lambda peer: scaled_copy(mine, peer).start())
    scaled_in[side, mine] = scaled_out[...]
    each_member(lambda peer: scaled_copy(peer, peer).wait_recv())
    swap = to_pair(scaled_in.at[side], scaled_in.at[side], 2)
    swap.start()

    def correction_of(which, where):
        scaled = scaled_in[which].reshape(every, half_rank)
        first = scaled.astype(jnp.bfloat16)
        rest = scaled - first.astype(jnp.float32)
        second = rest.astype(jnp.bfloat16)
        third = (rest - second.astype(jnp.float32)).astype(jnp.bfloat16)
        slots = members // 2
        factor_half = factor_in[pl.ds(which * slots, slots), :, span(where, width)].reshape(
            half_rank, width)
        return (
            jnp.dot(third, factor_half, preferred_element_type=jnp.float32)
            + jnp.dot(second, factor_half, preferred_element_type=jnp.float32)
        ) + jnp.dot(first, factor_half, preferred_element_type=jnp.float32)

    outgoing = correction_of(side, 1 - group)
    swap.wait()
    outgoing = outgoing + correction_of(1 - side, 1 - group)
    cross_out[...] = outgoing.reshape(2, half, width)
    for k in range(2):
        cross_copy(k).start()
    correction = correction_of(side, group) + correction_of(1 - side, group)
    query_own = query_in[:, :, span(group, width)].astype(jnp.float32).reshape(every, width)

    def finish_own(k):
        cross_copy(k).wait_recv()
        rows_of = slice(k * half, (k + 1) * half)
        whole = correction[rows_of] + cross_in[k]
        pre[me, rows_of] = ((query_own[rows_of] - whole) / damping[0]).astype(jnp.bfloat16)

    def scores_of(index):
        train_copy(index).wait()
        return lax.dot_general(
            pre[index], train_in[index], CONTRACT_LAST, preferred_element_type=jnp.float32)

    def height(i):
        mirror = lax.div(pz, line // 2)
        near = pz + mirror * (line - 1 - 2 * pz)
        v = near + i * (1 - 2 * near) if i < 2 else i
        return v + mirror * (line - 1 - 2 * v)

    def pass_on(z, k):
        @pl.when((z <= pz) & (pz < line - 1))
        def _():
            line_copy(z, k, 1).start()

        @pl.when((z >= pz) & (pz > 0))
        def _():
            line_copy(z, k, 0).start()

    total[...] = jnp.zeros_like(total)
    for e in range(2 * line + 2):
        if e < 2 * line:
            i, k = divmod(e, 2)
            z = height(i)
            if i > 0:
                line_copy(z, k, 1).wait_recv()
            else:
                finish_own(k)
            pass_on(z, k)
            side_copy(z, k, 0).start()
            side_copy(z, k, 1).start()
        if 1 <= e <= 2 * line:
            i, k = divmod(e - 1, 2)
            z = height(i)
            side_copy(z, k, 0, True).wait_recv()
            if k == 0:
                corner_copy(z, 1).start()
            side_copy(z, k, 1, True).wait_recv()
            if k == 1:
                corner_copy(z, 0).start()
        if e >= 2:
            i, k = divmod(e - 2, 2)
            z = height(i)
            corner_copy(z, 1 - k, True).wait_recv()
            if k == 1:
                for flip_x in (False, True):
                    for flip_y in (False, True):
                        total[...] += scores_of(block(z, flip_x, flip_y))

    other_rows = pl.ds(pl.multiple_of((1 - side) * half, half), half)
    own_rows = pl.ds(pl.multiple_of(side * half, half), half)
    last = to_pair(total.at[other_rows], total_in, 1)
    last.start()

    each_peer(lambda peer: query_copy(me, peer).wait_send())

    def finish(peer):
        factor_copy(mine, peer).wait_send()
        part_copy(mine, peer).wait_send()
        scaled_copy(mine, peer).wait_send()
    each_member(finish)
    for k in range(2):
        cross_copy(k).wait_send()
    for i in range(line):
        z = height(i)
        for k in range(2):
            @pl.when((z <= pz) & (pz < line - 1))
            def _():
                line_copy(z, k, 1).wait_send()

            @pl.when((z >= pz) & (pz > 0))
            def _():
                line_copy(z, k, 0).wait_send()

            for along in range(2):
                side_copy(z, k, along).wait_send()
        for along in range(2):
            corner_copy(z, along).wait_send()
    last.wait()
    out[...] = (total[own_rows, :] + total_in[...]).astype(out.dtype)


def fused(nb, queries, factor, eigenvalues, damping, train_rows):
    rows, depth = queries.shape
    rank_slice = factor.shape[1]
    width = depth // nb
    rank = eigenvalues.shape[0]
    every = nb * rows
    train = train_rows.shape[0]
    line = nb // 4
    members = nb // 2
    anywhere = pl.BlockSpec(memory_space=pl.ANY)
    vmem = pl.BlockSpec(memory_space=pltpu.VMEM)
    dma = pltpu.SemaphoreType.DMA
    f32, bf16 = jnp.float32, jnp.bfloat16
    return pl.pallas_call(
        functools.partial(fused_kernel, nb),
        out_shape=jax.ShapeDtypeStruct((every // 2, train), bf16),
        in_specs=[anywhere, anywhere, vmem, pl.BlockSpec(memory_space=pltpu.SMEM), anywhere],
        out_specs=vmem,
        scratch_shapes=[
            pltpu.VMEM((nb, rows, 2 * width), bf16),
            pltpu.VMEM((members, rank_slice, 2 * width), bf16),
            pltpu.VMEM((nb, train, width), bf16),
            pltpu.VMEM((2, members, 2 * rows, rank // 4), f32),
            pltpu.VMEM((members, 2 * rows, rank // 4), f32),
            pltpu.VMEM((members, 2 * rows, rank // 4), f32),
            pltpu.VMEM((members, 2 * rows, rank // 4), f32),
            pltpu.VMEM((2 * rows, rank // 4), f32),
            pltpu.VMEM((2, members, 2 * rows, rank // 4), f32),
            pltpu.VMEM((2, every // 2, width), f32),
            pltpu.VMEM((2, every // 2, width), f32),
            pltpu.VMEM((nb, every, width), bf16),
            pltpu.VMEM((every, train), f32),
            pltpu.VMEM((every // 2, train), f32),
            dma((nb,)), dma((2,)),
            dma((nb,)), dma((nb,)), dma((members,)), dma((members,)),
            dma((members,)), dma((members,)), dma((members,)), dma((members,)),
            dma((2, 2 * line)), dma((2 * line,)), dma((2, 2 * line)), dma((2, 2 * line)),
            dma((2, line)), dma((2, line)), dma((3,)), dma((3,)), dma((2,)), dma((2,)),
        ],
        compiler_params=pltpu.CompilerParams(
            collective_id=0, has_side_effects=True, vmem_limit_bytes=56 * 1024 * 1024),
    )(queries, factor.T, eigenvalues[None, :], damping, train_rows)


def plain(queries, factor, eigenvalues, damping, train_rows):
    damp_value = damping[0]
    weights = eigenvalues / (eigenvalues + damp_value)
    query_part = lax.all_to_all(queries, "blk", split_axis=1, concat_axis=0, tiled=True)
    factor_part = lax.all_to_all(factor, "blk", split_axis=0, concat_axis=1, tiled=True)
    partial_value = jnp.dot(query_part, factor_part, preferred_element_type=jnp.float32)
    coefficient = lax.psum(partial_value, ("blk", "col"))
    scaled = coefficient * weights[None, :]
    correction = jnp.dot(scaled, factor_part.astype(jnp.float32).T, precision=lax.Precision.HIGHEST)
    pre_part = ((query_part.astype(jnp.float32) - correction) / damp_value).astype(jnp.bfloat16)
    pre_all = lax.all_gather(pre_part, "blk", axis=1, tiled=True)
    partial_scores = jnp.einsum("qk,nk->qn", pre_all, train_rows, preferred_element_type=jnp.float32)
    scores = lax.psum_scatter(partial_scores, "col", scatter_dimension=0, tiled=True)
    return scores.astype(jnp.bfloat16)


def per_device(nb, pair, queries, factor, eigenvalues, damping, train_rows):
    rows, depth = queries.shape
    width = depth // nb
    fits = pair == 2 and width % 128 == 0 and eigenvalues.shape[0] % 512 == 0 and rows % 8 == 0 and factor.shape[1] % 16 == 0
    fits = fits and nb == 16
    if fits:
        return fused(nb, queries, factor, eigenvalues, damping, train_rows)
    return plain(queries, factor, eigenvalues, damping, train_rows)


def solution(mesh):
    in_specs = (P("blk", "col"), P("col", "blk"), P(), P(), P("blk", "col"))
    out_specs = P("col", "blk")
    body = functools.partial(per_device, mesh.shape["blk"], mesh.shape["col"])
    return jax.shard_map(
        body, mesh=mesh, in_specs=in_specs, out_specs=out_specs, check_vma=False
    )
```

```python
import functools

import jax
import jax.numpy as jnp
from jax import lax
from jax.experimental import pallas as pl
from jax.experimental.pallas import tpu as pltpu
from jax.sharding import PartitionSpec as P

MESH = pl.DeviceIdType.MESH
CONTRACT_LAST = (((1,), (1,)), ((), ()))


def fused_kernel(
    nb, queries, factor_t, eigenvalues, damping, train_rows, out,
    query_in, factor_in, train_in, part, pair_in, part_sum, part_in, scaled_out, scaled_in,
    cross_out, cross_in, pre, total, total_in,
    train_sem, own_sem, query_send, query_recv, factor_send, factor_recv,
    part_send, part_recv, scaled_send, scaled_recv, line_send, line_recv,
    side_send, side_recv, corner_send, corner_recv, pair_send, pair_recv, cross_send, cross_recv,
):
    me = lax.axis_index("blk")
    side = lax.axis_index("col")
    rows, wide = query_in.shape[1], query_in.shape[2]
    width = wide // 2
    rank = eigenvalues.shape[1]
    every = nb * rows
    half = every // 2
    members = nb // 2
    group, mine = lax.div(me, members), lax.rem(me, members)
    half_rank = rank // 4
    line = nb // 4
    px, py, pz = lax.rem(me, 2), lax.rem(lax.div(me, 2), 2), lax.div(me, 4)
    next_x = me + 1 - 2 * px
    next_y = me + 2 - 4 * py

    def span(index, size):
        return pl.ds(pl.multiple_of(index * size, size), size)

    def to_peer(source, target, send_sem, recv_sem, peer):
        return pltpu.make_async_remote_copy(
            src_ref=source, dst_ref=target, send_sem=send_sem, recv_sem=recv_sem,
            device_id={"blk": peer}, device_id_type=MESH,
        )

    def to_pair(source, target, index):
        return pltpu.make_async_remote_copy(
            src_ref=source, dst_ref=target,
            send_sem=pair_send.at[index], recv_sem=pair_recv.at[index],
            device_id={"col": 1 - side}, device_id_type=MESH,
        )

    def each_peer(body):
        def step(k, carry):
            body(lax.rem(me + k, nb))
            return carry
        lax.fori_loop(1, nb, step, 0)

    def each_member(body):
        def step(k, carry):
            body(mine + (k % 2) * (1 - 2 * lax.rem(mine, 2)) + 2 * (lax.rem(lax.div(k, 2), 2)) * (1 - 2 * lax.rem(lax.div(mine, 2), 2)) + 4 * lax.div(k, 4) * (1 - 2 * lax.div(mine, 4)))
            return carry
        lax.fori_loop(1, members, step, 0)

    def query_copy(source, peer):
        return to_peer(queries.at[:, span(lax.rem(peer, members), wide)], query_in.at[source],
                       query_send.at[peer], query_recv.at[source], peer)

    def factor_copy(source, member):
        return to_peer(factor_t.at[:, span(member, wide)], factor_in.at[source],
                       factor_send.at[member], factor_recv.at[source], group * members + member)

    def part_copy(source, member):
        return to_peer(part_sum.at[member], part_in.at[source],
                       part_send.at[member], part_recv.at[source], group * members + member)

    def scaled_copy(source, member):
        return to_peer(scaled_out, scaled_in.at[side, source],
                       scaled_send.at[member], scaled_recv.at[source], group * members + member)

    def cross_copy(k):
        return to_peer(cross_out.at[k], cross_in.at[k], cross_send.at[k], cross_recv.at[k],
                       (1 - group) * members + mine)

    def block(z, flip_x, flip_y):
        x = 1 - px if flip_x else px
        y = 1 - py if flip_y else py
        return z * 4 + y * 2 + x

    def line_copy(z, k, up):
        half_block = pre.at[block(z, False, False), pl.ds(k * half, half)]
        return to_peer(half_block, half_block, line_send.at[up, 2 * z + k],
                       line_recv.at[2 * z + k], me + (4 if up else -4))

    def side_copy(z, k, along, incoming=False):
        index = block(z, incoming and along == 0, incoming and along == 1)
        half_block = pre.at[index, pl.ds(k * half, half)]
        return to_peer(half_block, half_block, side_send.at[along, 2 * z + k],
                       side_recv.at[along, 2 * z + k], next_y if along else next_x)

    def corner_copy(z, along, incoming=False):
        index = block(z, incoming or along == 1, incoming or along == 0)
        half_block = pre.at[index, pl.ds((1 - along) * half, half)]
        return to_peer(half_block, half_block, corner_send.at[along, z],
                       corner_recv.at[along, z], next_y if along else next_x)

    def train_copy(index):
        chunk = lax.rem(index, members) * 2 + lax.div(index, members)
        return pltpu.make_async_copy(
            train_rows.at[:, span(chunk, width)], train_in.at[index], train_sem.at[index])

    own_query = pltpu.make_async_copy(
        queries.at[:, span(mine, wide)], query_in.at[me], own_sem.at[0])
    own_factor = pltpu.make_async_copy(
        factor_t.at[:, span(mine, wide)], factor_in.at[mine], own_sem.at[1])

    barrier = pltpu.get_barrier_semaphore()
    each_peer(lambda peer: pl.semaphore_signal(
        barrier, inc=1, device_id={"blk": peer}, device_id_type=MESH))
    pl.semaphore_signal(barrier, inc=1, device_id={"col": 1 - side}, device_id_type=MESH)
    pl.semaphore_wait(barrier, nb)

    own_query.start()
    own_factor.start()
    each_peer(lambda peer: query_copy(me, peer).start())
    each_member(lambda peer: factor_copy(mine, peer).start())

    def start_train(k, carry):
        train_copy(lax.rem(me + nb - k, nb)).start()
        return carry
    lax.fori_loop(0, nb, start_train, 0)

    own_query.wait()
    own_factor.wait()
    each_peer(lambda peer: query_copy(peer, peer).wait_recv())
    each_member(lambda peer: factor_copy(peer, peer).wait_recv())

    query_wide = query_in[...].astype(jnp.float32).reshape(every, wide)
    partial_value = lax.dot_general(
        query_wide.astype(jnp.bfloat16), factor_in[...].reshape(2 * half_rank, wide),
        CONTRACT_LAST, preferred_element_type=jnp.float32)
    for k in range(2):
        part[k] = partial_value[:, k * half_rank:(k + 1) * half_rank].reshape(
            members, 2 * rows, half_rank)

    exchange = to_pair(part.at[1 - side], pair_in, 0)
    exchange.start()
    own_rank = span(2 * group + side, half_rank)
    own_values = eigenvalues[:, own_rank]
    weights = own_values / (own_values + damping[0])
    exchange.wait()
    part_sum[...] = part[side] + pair_in[...]
    each_member(lambda peer: part_copy(mine, peer).start())
    part_in[mine] = part_sum[mine]
    each_member(lambda peer: part_copy(peer, peer).wait_recv())
    scaled_out[...] = jnp.sum(part_in[...], axis=0) * weights
    each_member(lambda peer: scaled_copy(mine, peer).start())
    scaled_in[side, mine] = scaled_out[...]
    each_member(lambda peer: scaled_copy(peer, peer).wait_recv())
    swap = to_pair(scaled_in.at[side], scaled_in.at[side], 2)
    swap.start()

    def correction_of(which, where):
        scaled = scaled_in[which].reshape(every, half_rank)
        first = scaled.astype(jnp.bfloat16)
        rest = scaled - first.astype(jnp.float32)
        second = rest.astype(jnp.bfloat16)
        third = (rest - second.astype(jnp.float32)).astype(jnp.bfloat16)
        slots = members // 2
        factor_half = factor_in[pl.ds(which * slots, slots), :, span(where, width)].reshape(
            half_rank, width)
        return (
            jnp.dot(third, factor_half, preferred_element_type=jnp.float32)
            + jnp.dot(second, factor_half, preferred_element_type=jnp.float32)
        ) + jnp.dot(first, factor_half, preferred_element_type=jnp.float32)

    outgoing = correction_of(side, 1 - group)
    swap.wait()
    outgoing = outgoing + correction_of(1 - side, 1 - group)
    cross_out[...] = outgoing.reshape(2, half, width)
    for k in range(2):
        cross_copy(k).start()
    correction = correction_of(side, group) + correction_of(1 - side, group)
    query_own = query_in[:, :, span(group, width)].astype(jnp.float32).reshape(every, width)

    def finish_own(k):
        cross_copy(k).wait_recv()
        rows_of = slice(k * half, (k + 1) * half)
        whole = correction[rows_of] + cross_in[k]
        pre[me, rows_of] = ((query_own[rows_of] - whole) / damping[0]).astype(jnp.bfloat16)

    def scores_of(index):
        train_copy(index).wait()
        return lax.dot_general(
            pre[index], train_in[index], CONTRACT_LAST, preferred_element_type=jnp.float32)

    def height(i):
        mirror = lax.div(pz, line // 2)
        near = pz + mirror * (line - 1 - 2 * pz)
        v = near + i * (1 - 2 * near) if i < 2 else i
        return v + mirror * (line - 1 - 2 * v)

    def pass_on(z, k):
        @pl.when((z <= pz) & (pz < line - 1))
        def _():
            line_copy(z, k, 1).start()

        @pl.when((z >= pz) & (pz > 0))
        def _():
            line_copy(z, k, 0).start()

    total[...] = jnp.zeros_like(total)
    side_lag, corner_lag = 3, 6

    def add_scores(z, flip_x, flip_y):
        total[...] += scores_of(block(z, flip_x, flip_y))

    for e in range(2 * line + corner_lag):
        if e < 2 * line:
            i, k = divmod(e, 2)
            z = height(i)
            if i > 0:
                line_copy(z, k, 1).wait_recv()
            else:
                finish_own(k)
            pass_on(z, k)
            side_copy(z, k, 0).start()
            side_copy(z, k, 1).start()
        if 0 <= e - side_lag < 2 * line:
            i, k = divmod(e - side_lag, 2)
            z = height(i)
            side_copy(z, k, k, True).wait_recv()
            corner_copy(z, 1 - k).start()
            if k == 1:
                side_copy(z, 1, 0, True).wait_recv()
                add_scores(z, True, False)
                side_copy(z, 0, 1, True).wait_recv()
                add_scores(z, False, True)
        if e < 2 * line and e % 2 == 1:
            add_scores(height(e // 2), False, False)
        if e >= corner_lag:
            i, k = divmod(e - corner_lag, 2)
            z = height(i)
            corner_copy(z, 1 - k, True).wait_recv()
            if k == 1:
                add_scores(z, True, True)

    other_rows = pl.ds(pl.multiple_of((1 - side) * half, half), half)
    own_rows = pl.ds(pl.multiple_of(side * half, half), half)
    last = to_pair(total.at[other_rows], total_in, 1)
    last.start()

    each_peer(lambda peer: query_copy(me, peer).wait_send())

    def finish(peer):
        factor_copy(mine, peer).wait_send()
        part_copy(mine, peer).wait_send()
        scaled_copy(mine, peer).wait_send()
    each_member(finish)
    for k in range(2):
        cross_copy(k).wait_send()
    for i in range(line):
        z = height(i)
        for k in range(2):
            @pl.when((z <= pz) & (pz < line - 1))
            def _():
                line_copy(z, k, 1).wait_send()

            @pl.when((z >= pz) & (pz > 0))
            def _():
                line_copy(z, k, 0).wait_send()

            for along in range(2):
                side_copy(z, k, along).wait_send()
        for along in range(2):
            corner_copy(z, along).wait_send()
    last.wait()
    out[...] = (total[own_rows, :] + total_in[...]).astype(out.dtype)


def fused(nb, queries, factor, eigenvalues, damping, train_rows):
    rows, depth = queries.shape
    rank_slice = factor.shape[1]
    width = depth // nb
    rank = eigenvalues.shape[0]
    every = nb * rows
    train = train_rows.shape[0]
    line = nb // 4
    members = nb // 2
    anywhere = pl.BlockSpec(memory_space=pl.ANY)
    vmem = pl.BlockSpec(memory_space=pltpu.VMEM)
    dma = pltpu.SemaphoreType.DMA
    f32, bf16 = jnp.float32, jnp.bfloat16
    return pl.pallas_call(
        functools.partial(fused_kernel, nb),
        out_shape=jax.ShapeDtypeStruct((every // 2, train), bf16),
        in_specs=[anywhere, anywhere, vmem, pl.BlockSpec(memory_space=pltpu.SMEM), anywhere],
        out_specs=vmem,
        scratch_shapes=[
            pltpu.VMEM((nb, rows, 2 * width), bf16),
            pltpu.VMEM((members, rank_slice, 2 * width), bf16),
            pltpu.VMEM((nb, train, width), bf16),
            pltpu.VMEM((2, members, 2 * rows, rank // 4), f32),
            pltpu.VMEM((members, 2 * rows, rank // 4), f32),
            pltpu.VMEM((members, 2 * rows, rank // 4), f32),
            pltpu.VMEM((members, 2 * rows, rank // 4), f32),
            pltpu.VMEM((2 * rows, rank // 4), f32),
            pltpu.VMEM((2, members, 2 * rows, rank // 4), f32),
            pltpu.VMEM((2, every // 2, width), f32),
            pltpu.VMEM((2, every // 2, width), f32),
            pltpu.VMEM((nb, every, width), bf16),
            pltpu.VMEM((every, train), f32),
            pltpu.VMEM((every // 2, train), f32),
            dma((nb,)), dma((2,)),
            dma((nb,)), dma((nb,)), dma((members,)), dma((members,)),
            dma((members,)), dma((members,)), dma((members,)), dma((members,)),
            dma((2, 2 * line)), dma((2 * line,)), dma((2, 2 * line)), dma((2, 2 * line)),
            dma((2, line)), dma((2, line)), dma((3,)), dma((3,)), dma((2,)), dma((2,)),
        ],
        compiler_params=pltpu.CompilerParams(
            collective_id=0, has_side_effects=True, vmem_limit_bytes=56 * 1024 * 1024),
    )(queries, factor.T, eigenvalues[None, :], damping, train_rows)


def plain(queries, factor, eigenvalues, damping, train_rows):
    damp_value = damping[0]
    weights = eigenvalues / (eigenvalues + damp_value)
    query_part = lax.all_to_all(queries, "blk", split_axis=1, concat_axis=0, tiled=True)
    factor_part = lax.all_to_all(factor, "blk", split_axis=0, concat_axis=1, tiled=True)
    partial_value = jnp.dot(query_part, factor_part, preferred_element_type=jnp.float32)
    coefficient = lax.psum(partial_value, ("blk", "col"))
    scaled = coefficient * weights[None, :]
    correction = jnp.dot(scaled, factor_part.astype(jnp.float32).T, precision=lax.Precision.HIGHEST)
    pre_part = ((query_part.astype(jnp.float32) - correction) / damp_value).astype(jnp.bfloat16)
    pre_all = lax.all_gather(pre_part, "blk", axis=1, tiled=True)
    partial_scores = jnp.einsum("qk,nk->qn", pre_all, train_rows, preferred_element_type=jnp.float32)
    scores = lax.psum_scatter(partial_scores, "col", scatter_dimension=0, tiled=True)
    return scores.astype(jnp.bfloat16)


def per_device(nb, pair, queries, factor, eigenvalues, damping, train_rows):
    rows, depth = queries.shape
    width = depth // nb
    fits = pair == 2 and width % 128 == 0 and eigenvalues.shape[0] % 512 == 0 and rows % 8 == 0 and factor.shape[1] % 16 == 0
    fits = fits and nb == 16
    if fits:
        return fused(nb, queries, factor, eigenvalues, damping, train_rows)
    return plain(queries, factor, eigenvalues, damping, train_rows)


def solution(mesh):
    in_specs = (P("blk", "col"), P("col", "blk"), P(), P(), P("blk", "col"))
    out_specs = P("col", "blk")
    body = functools.partial(per_device, mesh.shape["blk"], mesh.shape["col"])
    return jax.shard_map(
        body, mesh=mesh, in_specs=in_specs, out_specs=out_specs, check_vma=False
    )
```
